1024 devices in a mesh: rep: 32 (over y, x_hi, core), exp: 32 (over x_lo, z).
Axes of the slice: x: 8 (x_hi: 2, x_lo: 4; x = x_hi * 4 + x_lo), y: 8, z: 8, core: 2. Of those that a mesh axis runs over, the one named last changes fastest.
Arguments:
- replay_buffer_rows: bfloat16 [131072, 3584], P(('rep', 'exp')), may hold values from -6 to 6
- shard_request_index: int32 [1024, 32, 8], P(('rep', 'exp')), may hold values from 0 to 127
- replica_fetch_count: int32 [1024, 32], P(('rep', 'exp')), may hold values from 0 to 8, as said below
- routes: int32 [131072, 1], P(('rep', 'exp')), may hold values from 0 to 31; in each aligned block of 128 rows (0 to 127, 128 to 255, ...) at most 7 rows name the same one
- router_route_weight: float32 [131072, 1], P(('rep', 'exp')), may hold values from 0.25 to 1
- output_gradient: bfloat16 [131072, 1024], P(('rep', 'exp')), may hold values from -0.119628906 to 0.119628906
- frozen_gate_weight: bfloat16 [32, 3584, 1024], P('exp'), may hold values from -0.09375 to 0.09375
- adapter_down_weight: bfloat16 [32, 3584, 128], P('exp'), may hold values from -0.09375 to 0.09375
- adapter_up_weight: bfloat16 [32, 128, 1024], P('exp'), may hold values from -0.5 to 0.5
Outputs:
- out_rows: bfloat16 [131072, 1024], P(('rep', 'exp'))
- down_adapter_gradient: float32 [32, 3584, 128], P('exp', 'rep')
- up_adapter_gradient: float32 [32, 128, 1024], P('exp', 'rep')
The draws below stay inside these ranges and needn't reach their ends.
Inputs may be any that keep to these rules, and one draw needn't show every extreme that they name: Each row replica_fetch_count[d, :] sums to 128, and every row has an entry equal to 8. `shard_request_index`: entry [s * 32 + c, r, j] is read only where j < replica_fetch_count[r * 32 + c, s]. `routes`: among the 128 rows of one device no expert is named more than 7 times, and that bound is reached.
All inputs are finite; a program needn't handle non-finite values.
Results may differ from the reference program's by a relative error of at most 0.0061.
Values may be sent and summed in bfloat16 or wider, within the bound.
A program may use at most 64 MiB of HBM per device.

```python
import math
import jax
import jax.numpy as jnp
import numpy as np
from jax import lax

MODEL_DIM = 3584
HIDDEN_WIDTH = 1024
ADAPTER_RANK = 128
TOPK = 1
TOK_DEV = 128
BUF_DEV = 128
EXPERT_TOTAL = 32
TOKENS = 131072
BUF = 131072
FCAP = 8
CAP = 7
N_REP = 32
N_EXP = 32
DEVICES = 1024


def draw_replica_fetch_count(key, part):
    mean_count = TOK_DEV // N_REP
    half_count = N_REP // 2
    row_count = N_REP * N_EXP
    order_keys = jax.random.split(jax.random.fold_in(key, 11), row_count)
    orders = jax.vmap(lambda single: jax.random.permutation(single, N_REP))(order_keys).astype(jnp.int32)
    moves = jax.random.randint(jax.random.fold_in(key, 12), (row_count, half_count), 0, mean_count + 1).astype(jnp.int32)
    moves = moves.at[:, 0].set(mean_count)
    values = jnp.concatenate([mean_count + moves, mean_count - moves], axis=1).astype(jnp.int32)
    row_index = jnp.broadcast_to(jnp.arange(row_count, dtype=jnp.int32)[:, None], (row_count, N_REP))
    counts = jnp.zeros((row_count, N_REP), jnp.int32).at[row_index, orders].set(values)
    return counts


def place_ends(entries, rng, smallest, top_value):
    longest = entries.shape.index(max(entries.shape))
    spots = []
    for shift in (0, 1):
        where = [jax.random.randint(jax.random.fold_in(rng, axis), (), 0, length) for axis, length in enumerate(entries.shape)]
        where[longest] = (where[longest] + shift) % entries.shape[longest]
        spots.append(tuple(where))
    return entries.at[spots[0]].set(smallest).at[spots[1]].set(top_value)


def level_of(rng, shape, pieces, least, top_value):
    def one(position, shards_of):
        steps = jax.random.uniform(jax.random.fold_in(jax.random.fold_in(rng, 6), position), (shards_of,), jnp.float32, least / len(pieces), top_value / len(pieces))
        return jnp.repeat(jnp.exp(steps), shape[position] // shards_of).reshape((-1,) + (1,) * (len(shape) - position - 1))

    level = one(*pieces[0])
    for cut in pieces[1:]:
        level = level * one(*cut)
    return level


def routed_block(rng, own, number, rows, count, top, reach, skew):
    order = jax.random.permutation(rng, count)
    packed, usual = shares(count, rows * top, reach, skew, True), shares(count, rows * top, reach, skew, False)
    places = jnp.arange(count)

    def named(sizes, turn):
        used = int((sizes > 0).sum())
        fixed = max(1, used // 4)
        passed = fixed + (places - fixed + turn * (used - fixed)) % max(1, count - fixed)
        return jnp.zeros((count,), jnp.int32).at[order[jnp.where(places < fixed, places, passed)]].set(jnp.asarray(sizes, jnp.int32))

    sizes = jnp.where(number % 4 == 0, named(packed, number // 4), named(usual, number - number // 4 - 1))
    mixed = jax.random.permutation(jax.random.fold_in(own, 3), count)
    donor, receiver = mixed[0:count // 2 * 2:2], mixed[1:count // 2 * 2:2]
    margin = jnp.minimum(sizes[donor] - 1, reach - sizes[receiver]) // 2
    margin = jnp.where((donor == order[0]) | (receiver == order[0]) | (sizes[receiver] == 0), 0, jnp.maximum(margin, 0))
    passed = jax.random.randint(jax.random.fold_in(own, 4), (count // 2,), 0, 1 << 20) % (margin + 1)
    sizes = sizes.at[donor].add(-passed).at[receiver].add(passed)
    items = jnp.searchsorted(jnp.cumsum(sizes), jnp.arange(rows * top), side="right").astype(jnp.int32)
    listing = items.reshape(top, rows).T
    listing = listing[jax.random.permutation(jax.random.fold_in(own, 1), rows)]
    turn = jax.random.randint(jax.random.fold_in(own, 2), (rows, 1), 0, top)
    return jnp.take_along_axis(listing, (jnp.arange(top)[None, :] + turn) % top, axis=1)


def shares(number_of, total, most, slope, full):
    portions = [(1 << 20) // math.isqrt(standing ** slope) + 1 for standing in range(1, number_of + 1)]
    largest = most if full else min(most, max(-(-total // number_of), total * portions[0] // sum(portions)))
    least = 1 if total - largest >= number_of - 1 else 0
    given, rest = [largest] + [least] * (number_of - 1), total - largest - least * (number_of - 1)
    while rest > 0:
        free = [i for i in range(1, number_of) if given[i] < largest] or [i for i in range(1, number_of) if given[i] < most]
        mass, budget = sum([portions[i] for i in free]), rest
        for i in free:
            addition = min(most - given[i], max(1, budget * portions[i] // mass), rest)
            given[i] = given[i] + addition
            rest = rest - addition
    return np.array(given)


def noise(key, shape, width, reach, pieces=(), kind=jnp.bfloat16):
    result = width * jax.random.normal(key, shape, jnp.float32)
    if pieces:
        result = result * level_of(key, shape, pieces, -0.22, 0.18)
    return jnp.clip(result, -reach, reach).astype(kind)


def setup_inputs(seed: int = 0) -> dict:
    seeds = jax.random.split(jax.random.key(seed), 10)
    replay_buffer_rows = noise(seeds[0], (BUF, MODEL_DIM), 1.0, 6.0, ((0, 1024),))
    shard_request_index = place_ends(jax.random.randint(seeds[1], (DEVICES, N_REP, FCAP), 0, BUF_DEV), jax.random.fold_in(seeds[1], 1), 0, BUF_DEV - 1).astype(jnp.int32)
    replica_fetch_count = draw_replica_fetch_count(jax.random.fold_in(seeds[9], 71), 0)
    routes_keys = jax.random.split(jax.random.fold_in(seeds[3], 1), TOKENS // TOK_DEV)
    routes_turns = jax.random.permutation(jax.random.fold_in(seeds[3], 3), TOKENS // TOK_DEV)
    routes = jax.vmap(lambda own, number: routed_block(jax.random.fold_in(seeds[3], 2), own, number, TOK_DEV, EXPERT_TOTAL, TOPK, CAP, 2))(routes_keys, routes_turns).reshape((TOKENS, TOPK))
    router_route_weight = jnp.clip(0.25 + 0.75 * jax.random.uniform(seeds[4], (TOKENS, TOPK), jnp.float32) ** level_of(seeds[4], (TOKENS, TOPK), ((0, 1024),), -0.2, 0.2), 0.25, 1.0)
    output_gradient = noise(seeds[5], (TOKENS, HIDDEN_WIDTH), 0.02, 0.119628906, ((0, 1024),))
    frozen_gate_weight = noise(seeds[6], (EXPERT_TOTAL, MODEL_DIM, HIDDEN_WIDTH), MODEL_DIM ** -0.5, 0.09375, ((0, 32),))
    adapter_down_weight = noise(seeds[7], (EXPERT_TOTAL, MODEL_DIM, ADAPTER_RANK), MODEL_DIM ** -0.5, 0.09375, ((0, 32),))
    adapter_up_weight = noise(seeds[8], (EXPERT_TOTAL, ADAPTER_RANK, HIDDEN_WIDTH), ADAPTER_RANK ** -0.5, 0.5, ((0, 32),))
    return dict(replay_buffer_rows=replay_buffer_rows, shard_request_index=shard_request_index, replica_fetch_count=replica_fetch_count, routes=routes, router_route_weight=router_route_weight, output_gradient=output_gradient, frozen_gate_weight=frozen_gate_weight, adapter_down_weight=adapter_down_weight, adapter_up_weight=adapter_up_weight)


def silu_slope(pre_act):
    gate_value = jax.nn.sigmoid(pre_act)
    return gate_value * (1.0 + pre_act * (1.0 - gate_value))


def reference(replay_buffer_rows, shard_request_index, replica_fetch_count, routes, router_route_weight, output_gradient, frozen_gate_weight, adapter_down_weight, adapter_up_weight):
    device_count = N_REP * N_EXP
    row_ends = jnp.cumsum(replica_fetch_count, axis=1).astype(jnp.int32)
    row_starts = (row_ends - replica_fetch_count).astype(jnp.int32)
    positions = jnp.arange(TOK_DEV, dtype=jnp.int32)
    source = jnp.sum((row_ends[:, None, :] <= positions[None, :, None]).astype(jnp.int32), axis=2).astype(jnp.int32)
    offset = (positions[None, :] - jnp.take_along_axis(row_starts, source, axis=1)).astype(jnp.int32)
    device_ids = jnp.arange(device_count, dtype=jnp.int32)
    replica = device_ids // N_EXP
    column = device_ids % N_EXP
    server = (source * N_EXP + column[:, None]).astype(jnp.int32)
    local_row = shard_request_index[server, replica[:, None], offset]
    global_row = (server * BUF_DEV + local_row).reshape(-1).astype(jnp.int32)
    tokens = jnp.take(replay_buffer_rows, global_row, axis=0)

    slot_count = TOKENS * TOPK
    block_routes = routes.reshape(device_count, TOK_DEV * TOPK)
    expert_ids = jnp.arange(EXPERT_TOTAL, dtype=jnp.int32)
    chosen = (block_routes[:, :, None] == expert_ids[None, None, :]).astype(jnp.int32)
    slot_rank = jnp.sum((jnp.cumsum(chosen, axis=1) - 1) * chosen, axis=2).astype(jnp.int32)
    slot_device = jnp.repeat(device_ids, TOK_DEV * TOPK)
    slot_replica = (slot_device // N_EXP).astype(jnp.int32)
    slot_column = (slot_device % N_EXP).astype(jnp.int32)
    flat_expert = routes.reshape(-1).astype(jnp.int32)
    tile_pos = (slot_column * CAP + slot_rank.reshape(-1)).astype(jnp.int32)
    lookup_table = jnp.full((EXPERT_TOTAL, N_REP, N_EXP * CAP), slot_count, jnp.int32)
    lookup_table = lookup_table.at[flat_expert, slot_replica, tile_pos].set(jnp.arange(slot_count, dtype=jnp.int32))

    token_pad = jnp.concatenate([tokens, jnp.zeros((1, MODEL_DIM), jnp.bfloat16)], axis=0)
    slot_grad = (router_route_weight.reshape(-1, 1) * jnp.repeat(output_gradient, TOPK, axis=0).astype(jnp.float32)).astype(jnp.bfloat16)
    grad_pad = jnp.concatenate([slot_grad, jnp.zeros((1, HIDDEN_WIDTH), jnp.bfloat16)], axis=0)
    tile_len = N_EXP * CAP

    def single_expert_step(inputs):
        slot_ids, weight, down_map, up_map = inputs
        flat_ids = slot_ids.reshape(-1)
        token_ids = jnp.where(flat_ids < slot_count, flat_ids // TOPK, TOKENS).astype(jnp.int32)
        rows_x = jnp.take(token_pad, token_ids, axis=0)
        adapted_hidden = jnp.dot(rows_x, down_map, preferred_element_type=jnp.float32).astype(jnp.bfloat16)
        pre_act = jnp.dot(rows_x, weight, preferred_element_type=jnp.float32) + jnp.dot(adapted_hidden, up_map, preferred_element_type=jnp.float32)
        activated = jax.nn.silu(pre_act).astype(jnp.bfloat16)
        grad_rows = jnp.take(grad_pad, flat_ids, axis=0)
        preact_gradient = (grad_rows.astype(jnp.float32) * silu_slope(pre_act)).astype(jnp.bfloat16)
        back_reduced = jnp.dot(preact_gradient, up_map.T, preferred_element_type=jnp.float32).astype(jnp.bfloat16)
        shaped_x = rows_x.reshape(N_REP, tile_len, MODEL_DIM).astype(jnp.float32)
        shaped_back = back_reduced.reshape(N_REP, tile_len, ADAPTER_RANK).astype(jnp.float32)
        down_parts = jnp.einsum("rmd,rmk->rdk", shaped_x, shaped_back, precision=lax.Precision.HIGHEST)
        shaped_adapted = adapted_hidden.reshape(N_REP, tile_len, ADAPTER_RANK).astype(jnp.float32)
        shaped_grad = preact_gradient.reshape(N_REP, tile_len, HIDDEN_WIDTH).astype(jnp.float32)
        up_parts = jnp.einsum("rmk,rmf->rkf", shaped_adapted, shaped_grad, precision=lax.Precision.HIGHEST)
        down_sum = jnp.sum(down_parts, axis=0)
        up_sum = jnp.sum(up_parts, axis=0)
        return activated, down_sum, up_sum

    activated_rows_full, down_adapter_gradient, up_adapter_gradient = lax.map(single_expert_step, (lookup_table, frozen_gate_weight, adapter_down_weight, adapter_up_weight))
    slot_values = jnp.zeros((slot_count + 1, HIDDEN_WIDTH), jnp.bfloat16).at[lookup_table.reshape(-1)].set(activated_rows_full.reshape(-1, HIDDEN_WIDTH))
    slot_values = slot_values[:slot_count].reshape(TOKENS, TOPK, HIDDEN_WIDTH).astype(jnp.float32)
    out_rows = jnp.sum(router_route_weight[:, :, None] * slot_values, axis=1).astype(jnp.bfloat16)
    return out_rows, down_adapter_gradient, up_adapter_gradient
```

```python
import jax
import jax.numpy as jnp
from jax import lax
from jax.sharding import PartitionSpec as P

CAPACITY = 7
LANES = 128


def silu_slope(pre_act):
    gate_value = jax.nn.sigmoid(pre_act)
    return gate_value * (1.0 + pre_act * (1.0 - gate_value))


def body(
    replay_buffer_rows,
    shard_request_index,
    replica_fetch_count,
    routes,
    router_route_weight,
    output_gradient,
    frozen_gate_weight,
    adapter_down_weight,
    adapter_up_weight,
):
    rep_count = lax.axis_size("rep")
    exp_count = lax.axis_size("exp")
    token_count = routes.shape[0]
    fetch_slots = shard_request_index.shape[2]
    model_width = replay_buffer_rows.shape[1]
    hidden_units = frozen_gate_weight.shape[2]
    rank = adapter_down_weight.shape[2]
    tile_rows = exp_count * CAPACITY

    served = jnp.take(replay_buffer_rows, shard_request_index[0], axis=0)
    arrived = lax.all_to_all(served, "rep", split_axis=0, concat_axis=0, tiled=True)
    flat_rows = arrived.reshape(rep_count * fetch_slots, model_width)

    counts = replica_fetch_count[0]
    row_ends = jnp.cumsum(counts)
    row_starts = row_ends - counts
    positions = jnp.arange(token_count, dtype=jnp.int32)
    passed = (row_ends[None, :] <= positions[:, None]).astype(jnp.int32)
    source = jnp.sum(passed, axis=1)
    start_of = jnp.sum(passed * counts[None, :], axis=1)
    place = source * fetch_slots + positions - start_of
    expert_ids = lax.broadcasted_iota(jnp.int32, (token_count, exp_count), 1)
    chosen = (routes == expert_ids).astype(jnp.int32)
    slot_rank = jnp.sum((jnp.cumsum(chosen, axis=0) - 1) * chosen, axis=1)
    target = routes[:, 0] * CAPACITY + slot_rank
    row_ids = lax.broadcasted_iota(jnp.int32, (tile_rows, token_count), 0)
    picker = (row_ids == target[None, :]).astype(jnp.bfloat16)
    place_ids = lax.broadcasted_iota(jnp.int32, (token_count, rep_count * fetch_slots), 1)
    finder = (place_ids == place[:, None]).astype(jnp.bfloat16)
    mover = jnp.dot(picker, finder, preferred_element_type=jnp.float32).astype(jnp.bfloat16)

    scaled = (router_route_weight * output_gradient.astype(jnp.float32)).astype(jnp.bfloat16)
    grad_slots = jnp.dot(picker, scaled, preferred_element_type=jnp.float32).astype(jnp.bfloat16)
    row_slots = jnp.dot(mover, flat_rows, preferred_element_type=jnp.float32).astype(jnp.bfloat16)
    packed = jnp.concatenate([row_slots, grad_slots], axis=1)
    packed = packed.reshape(exp_count, CAPACITY, model_width + hidden_units)
    tile_in = lax.all_to_all(packed, "exp", split_axis=0, concat_axis=0, tiled=True)
    tile_in = tile_in.reshape(tile_rows, model_width + hidden_units)
    input_tile = tile_in[:, :model_width]
    grad_tile = tile_in[:, model_width:]

    adapted_hidden = jnp.dot(
        input_tile, adapter_down_weight[0], preferred_element_type=jnp.float32
    ).astype(jnp.bfloat16)
    pre_act = jnp.dot(
        input_tile, frozen_gate_weight[0], preferred_element_type=jnp.float32
    ) + jnp.dot(adapted_hidden, adapter_up_weight[0], preferred_element_type=jnp.float32)
    activated = jax.nn.silu(pre_act).astype(jnp.bfloat16)
    results = lax.all_to_all(
        activated.reshape(exp_count, CAPACITY, hidden_units),
        "exp",
        split_axis=0,
        concat_axis=0,
        tiled=True,
    )
    result_rows = results.reshape(tile_rows, hidden_units)
    picked = jnp.take(result_rows, target, axis=0).astype(jnp.float32)
    out_rows = (router_route_weight * picked).astype(jnp.bfloat16)

    preact_gradient = (grad_tile.astype(jnp.float32) * silu_slope(pre_act)).astype(jnp.bfloat16)
    up_term = lax.dot_general(
        adapted_hidden,
        preact_gradient,
        (((0,), (0,)), ((), ())),
        preferred_element_type=jnp.float32,
    )
    back_reduced = lax.dot_general(
        preact_gradient,
        adapter_up_weight[0],
        (((1,), (1,)), ((), ())),
        preferred_element_type=jnp.float32,
    ).astype(jnp.bfloat16)
    down_term = lax.dot_general(
        input_tile, back_reduced, (((0,), (0,)), ((), ())), preferred_element_type=jnp.float32
    )
    down_rows = model_width // rep_count
    up_rows = rank // rep_count
    up_tiles = up_rows * hidden_units // LANES
    terms = jnp.concatenate(
        [
            down_term.astype(jnp.bfloat16).reshape(rep_count, down_rows, rank),
            up_term.astype(jnp.bfloat16).reshape(rep_count, up_tiles, LANES),
        ],
        axis=1,
    )
    landed = lax.all_to_all(terms, "rep", split_axis=0, concat_axis=0, tiled=True)
    total = jnp.sum(landed.astype(jnp.float32), axis=0)
    down_grad = total[:down_rows].reshape(1, down_rows, rank)
    up_grad = total[down_rows:].reshape(1, up_rows, hidden_units)
    return (out_rows, down_grad, up_grad)


def solution(mesh):
    placed = (
        P(("rep", "exp"), None),
        P(("rep", "exp"), None, None),
        P(("rep", "exp"), None),
        P(("rep", "exp"), None),
        P(("rep", "exp"), None),
        P(("rep", "exp"), None),
        P("exp", None, None),
        P("exp", None, None),
        P("exp", None, None),
    )
    return jax.shard_map(
        body,
        mesh=mesh,
        in_specs=placed,
        out_specs=(P(("rep", "exp"), None), P("exp", "rep", None), P("exp", "rep", None)),
        check_vma=False,
    )
```
